32 devices in a mesh: tm: 4 (over z), space: 8 (over y, x, core).
Axes of the slice: x: 2, y: 2, z: 4, core: 2. Of those that a mesh axis runs over, the one named last changes fastest.
Arguments:
- iterate: float32 [4, 8, 16, 16, 512], P('tm', 'space'), may hold values from -3 to 3
- source_term: float32 [4, 8, 16, 16, 512], P('tm', 'space'), may hold values from -6 to 6
- conductivity: float32 [8, 16, 16, 512], P('space'), may hold values from 0.5 to 4
Outputs:
- new_iterate: float32 [4, 8, 16, 16, 512], P('tm', 'space')
- residual: float32 [4, 8, 16, 16, 512], P('tm', 'space')
The draws below stay inside these ranges and needn't reach their ends.
All inputs are finite; a program needn't handle non-finite values.
Results may differ from the reference program's by a relative error of at most 0.00002.
Values sent between devices are 32-bit elements; how exact they have to be, the bound alone decides.
A program may use at most 64 MiB of HBM per device.

```python
import math
import jax
import jax.numpy as jnp

NZ = 16
TX = 16
TY = 512
TILES = 8
NT = 4
N_SPACE = 8


def level_of(own_key, dims, split, smallest, top_value):
    def one(dim, parts):
        draws = jax.random.uniform(jax.random.fold_in(jax.random.fold_in(own_key, 6), dim), (parts,), jnp.float32, smallest / len(split), top_value / len(split))
        return jnp.repeat(jnp.exp(draws), dims[dim] // parts).reshape((-1,) + (1,) * (len(dims) - dim - 1))

    factor_of = one(*split[0])
    for cut in split[1:]:
        factor_of = factor_of * one(*cut)
    return factor_of


def bell_draw(own_key, extent, scale, most, split=(), dtype=jnp.bfloat16):
    loudness = level_of(own_key, extent, split, -0.22, 0.18) if split else 1.0
    array = jax.random.normal(own_key, extent, jnp.float32) * scale * loudness
    return jnp.minimum(jnp.maximum(array, -most), most).astype(dtype)


def setup_inputs(seed: int = 0) -> dict:
    key_of = jax.random.split(jax.random.key(seed), 4)
    return {
        "iterate": bell_draw(key_of[0], (NT, TILES, NZ, TX, TY), 0.6, 3.0, ((0, 4), (1, 8)), jnp.float32),
        "source_term": bell_draw(key_of[1], (NT, TILES, NZ, TX, TY), 1.0, 6.0, ((0, 4), (1, 8)), jnp.float32),
        "conductivity": jnp.clip(jnp.exp(math.log(4.0) - 2.0794415 * jax.random.uniform(key_of[2], (TILES, NZ, TX, TY), jnp.float32) ** level_of(key_of[2], (TILES, NZ, TX, TY), ((0, 8),), -0.2, 0.2)), 0.5, 4.0),
    }


tau_step = 0.08
damping = 0.7


def to_grid(tiled):
    frames = tiled.shape[0]
    return tiled.transpose(0, 2, 1, 3, 4).reshape(frames, NZ, N_SPACE * TX, TY)


def from_grid(grid_field):
    frames = grid_field.shape[0]
    shaped = grid_field.reshape(frames, NZ, N_SPACE, TX, TY)
    return shaped.transpose(0, 2, 1, 3, 4)


def neighbours(grid_field):
    padded = jnp.pad(grid_field, ((0, 0), (1, 1), (1, 1), (1, 1)))
    return [padded[:, 1:-1, :-2, 1:-1], padded[:, 1:-1, 2:, 1:-1],
            padded[:, 1:-1, 1:-1, :-2], padded[:, 1:-1, 1:-1, 2:],
            padded[:, :-2, 1:-1, 1:-1], padded[:, 2:, 1:-1, 1:-1]]


def face_weights(conduct):
    weights = [0.5 * (conduct + other) for other in neighbours(conduct)]
    weight_sum = weights[0]
    for near_item in weights[1:]:
        weight_sum = weight_sum + near_item
    return weights, weight_sum


def earlier(grid_field):
    return jnp.concatenate([jnp.zeros_like(grid_field[:1]), grid_field[:-1]], axis=0)


def apply_operator(update, weights, weight_sum, step_size):
    near_list = neighbours(update)
    flux_sum = weights[0] * near_list[0]
    for position in range(1, 6):
        flux_sum = flux_sum + weights[position] * near_list[position]
    return update - earlier(update) + step_size * (weight_sum * update - flux_sum)


def smooth(rhs_field, weights, weight_sum, step_size, want_left):
    diag_term = 1.0 + step_size * weight_sum
    update = damping * rhs_field / diag_term
    update = update + damping * (rhs_field - apply_operator(update, weights, weight_sum, step_size)) / diag_term
    if want_left:
        return update, rhs_field - apply_operator(update, weights, weight_sum, step_size)
    return update, update


def reference(iterate, source_term, conductivity):
    state_grid = to_grid(iterate)
    source_grid = to_grid(source_term)
    kappa_grid = to_grid(conductivity[None])
    conduct = kappa_grid * (1.0 + state_grid * state_grid)
    weights, weight_sum = face_weights(conduct)
    residual = source_grid - apply_operator(state_grid, weights, weight_sum, tau_step)
    fine_update, fine_left = smooth(residual, weights, weight_sum, tau_step, True)
    mid_rhs = fine_left[0::2] + fine_left[1::2]
    mid_conduct = 0.5 * (conduct[0::2] + conduct[1::2])
    weights, weight_sum = face_weights(mid_conduct)
    mid_update, mid_left = smooth(mid_rhs, weights, weight_sum, 2.0 * tau_step, True)
    top_rhs = mid_left[0::2] + mid_left[1::2]
    top_conduct = 0.5 * (mid_conduct[0::2] + mid_conduct[1::2])
    weights, weight_sum = face_weights(top_conduct)
    top_update, unused = smooth(top_rhs, weights, weight_sum, 4.0 * tau_step, False)
    mid_update = mid_update + jnp.repeat(top_update, 2, axis=0)
    fine_update = fine_update + jnp.repeat(mid_update, 2, axis=0)
    return from_grid(state_grid + fine_update), from_grid(residual)
```

```python
import functools

import jax
import jax.numpy as jnp
from jax import lax
from jax.experimental import pallas as pl
from jax.experimental.pallas import tpu as pltpu
from jax.sharding import PartitionSpec as P

tau_step = 0.08
damping = 0.7
group = 4
pad = 8
mesh_ids = pl.DeviceIdType.MESH

slots_state = [0, 2, 4, 6]
slots_one = [8, 9, 10, 11]
slots_two = [12, 13, 14, 15]
slots_mid_one = [16, 17]
slots_mid_two = [18, 19]
slot_top = 20
n_slots = 21


def kernel(
    tm_size, space_size,
    state_in, source_in, kappa_in, new_out, res_out,
    u, c, e1, e2, kap, src, res, wl, wr, rd,
    mc, me1, me2, mb, mwl, mwr, mrd, tc, te, tb, new,
    row_send, row_recv, col_send, col_recv,
    in_ssem, in_rsem, out_ssem, out_rsem, loc_sem, h_ssem, h_rsem, t_ssem, t_rsem,
):
    nz, tx, width = kap.shape
    real = pl.ds(pad, tx)
    low = pl.ds(pad - 1, tx)
    high = pl.ds(pad + 1, tx)
    planes = pl.ds(1, nz)
    me = lax.axis_index("tm")
    sp = lax.axis_index("space")
    q = me % group
    base = me - q
    chained = tm_size > group
    has_dn, has_up = sp > 0, sp < space_size - 1
    has_left, has_right = q > 0, q < group - 1
    has_prev, has_next = base > 0, base + group < tm_size
    sides = [
        (has_dn, {"space": sp - 1}),
        (has_up, {"space": sp + 1}),
        (has_left, {"tm": me - 1}),
        (has_right, {"tm": me + 1}),
    ]

    def zero_edges(ref, count):
        for n in range(count):
            for plane in (0, nz + 1):
                ref[n, plane] = jnp.zeros(ref.shape[2:], jnp.float32)

    zero_edges(u, group + 1)
    zero_edges(c, group)
    zero_edges(e1, group + 1)
    zero_edges(e2, group + 1)
    zero_edges(mc, 2)
    zero_edges(me1, 3)
    zero_edges(me2, 3)
    zero_edges(tc, 1)
    zero_edges(te, 2)

    @pl.when(jnp.logical_not(has_prev))
    def _():
        for ref in (u, e1, e2, me1, me2, te):
            ref[0] = jnp.zeros(ref.shape[1:], jnp.float32)

    for number, (has, _) in enumerate(sides):
        buffer = row_recv if number < 2 else col_recv

        @pl.when(jnp.logical_not(has))
        def _():
            buffer[number % 2] = jnp.zeros(buffer.shape[1:], jnp.float32)

    barrier = pltpu.get_barrier_semaphore()
    for j in range(1, group):
        pl.semaphore_signal(
            barrier, inc=1, device_id={"tm": base + (q + j) % group}, device_id_type=mesh_ids
        )
    greeted = [(has_dn, sides[0][1]), (has_up, sides[1][1])]
    if chained:
        greeted += [(has_prev, {"tm": me - group}), (has_next, {"tm": me + group})]
    for has, where in greeted:

        @pl.when(has)
        def _():
            pl.semaphore_signal(barrier, inc=1, device_id=where, device_id_type=mesh_ids)

    expected = group - 1
    for has, _ in greeted:
        expected = expected + jnp.where(has, 1, 0)
    pl.semaphore_wait(barrier, expected)

    def columns(d):
        return pl.ds(pl.multiple_of(d * width, width), width)

    def in_copy(a, j):
        d = (q + j) % group
        hbm = (state_in, source_in)[a].at[0, 0, :, :, columns(d)]
        dst = u.at[q + 1, planes, real, :] if a == 0 else src.at[q]
        if j == 0:
            return pltpu.make_async_copy(hbm, dst, loc_sem.at[a])
        return pltpu.make_async_remote_copy(
            src_ref=hbm, dst_ref=dst, send_sem=in_ssem.at[a, j - 1],
            recv_sem=in_rsem.at[a, j - 1], device_id={"tm": base + d}, device_id_type=mesh_ids,
        )

    def out_copy(a, j):
        d = (q + j) % group
        hbm = (res_out, new_out)[a].at[0, 0, :, :, columns(q)]
        own = (res, new)[a].at[d]
        if j == 0:
            return pltpu.make_async_copy(own, hbm, loc_sem.at[3 + a])
        return pltpu.make_async_remote_copy(
            src_ref=own, dst_ref=hbm, send_sem=out_ssem.at[a, j - 1],
            recv_sem=out_rsem.at[a, j - 1], device_id={"tm": base + d}, device_id_type=mesh_ids,
        )

    kappa_copy = pltpu.make_async_copy(
        kappa_in.at[0, :, :, columns(q)], kap, loc_sem.at[2]
    )
    kappa_copy.start()
    order = (2, 1, 3, 0)
    for a in range(2):
        for j in order:
            in_copy(a, j).start()

    def halo_copy(slot, count, number):
        part = pl.ds(slot, count)
        opposite = number ^ 1
        if number < 2:
            source, target = row_send.at[number, part], row_recv.at[opposite, part]
        else:
            source, target = col_send.at[part], col_recv.at[opposite - 2, part]
        return pltpu.make_async_remote_copy(
            src_ref=source, dst_ref=target, send_sem=h_ssem.at[number, slot],
            recv_sem=h_rsem.at[opposite, slot], device_id=sides[number][1],
            device_id_type=mesh_ids,
        )

    def halo_send(slot, count=1):
        for number in (2, 3, 0, 1):

            @pl.when(sides[number][0])
            def _():
                halo_copy(slot, count, number).start()

    def halo_wait(slot, count=1):
        part = pl.ds(slot, count)
        for number in range(4):
            target = row_recv.at[number, part] if number < 2 else col_recv.at[number - 2, part]

            @pl.when(sides[number][0])
            def _():
                pltpu.make_async_remote_copy(
                    src_ref=target, dst_ref=target, send_sem=h_ssem.at[number, slot],
                    recv_sem=h_rsem.at[number, slot], device_id=sides[number][1],
                    device_id_type=mesh_ids,
                ).wait_recv()

    def time_copy(number, ref, last):
        return pltpu.make_async_remote_copy(
            src_ref=ref.at[last, planes, real, :], dst_ref=ref.at[0, planes, real, :],
            send_sem=t_ssem.at[number],
            recv_sem=t_rsem.at[number], device_id={"tm": me + group}, device_id_type=mesh_ids,
        )

    time_refs = [(u, group), (e1, group), (e2, group), (me1, 2), (me2, 2), (te, 1)]

    def time_send(number):
        if chained:

            @pl.when(has_next)
            def _():
                time_copy(number, *time_refs[number]).start()

    def time_wait(number):
        if chained:

            @pl.when(has_prev)
            def _():
                time_copy(number, *time_refs[number]).wait_recv()

    lane = lax.broadcasted_iota(jnp.int32, (tx, width), 1)
    first_lane = lane == 0
    last_lane = lane == width - 1
    odd_lane = lane % 2 == 1
    pair_lane = lane // 2

    def pack(slot, p, value, packed):
        row_send[0, slot, pl.ds(p, 1), :] = value[:1]
        row_send[1, slot, pl.ds(p, 1), :] = value[tx - 1 :]
        return jnp.where(pair_lane == p, pltpu.roll(value, 2 * p + 1, 1), packed)

    def ghosts(slot):
        return jnp.where(
            odd_lane,
            pltpu.roll(col_recv[0, slot], 1, 1),
            pltpu.roll(col_recv[1, slot], width - 1, 1),
        )

    def put_rows(ref, n, slot, p):
        ref[n, p + 1, pl.ds(pad - 1, 1), :] = row_recv[0, slot, pl.ds(p, 1), :]
        ref[n, p + 1, pl.ds(pad + tx, 1), :] = row_recv[1, slot, pl.ds(p, 1), :]

    def sideways(value, ghost, p):
        edge = pltpu.roll(ghost, width - 1 - 2 * p, 1)
        left = jnp.where(first_lane, edge, pltpu.roll(value, 1, 1))
        right = jnp.where(last_lane, edge, pltpu.roll(value, width - 1, 1))
        return left, right

    def straight(ref, n, p):
        return (
            ref[n, p + 1, low, :], ref[n, p + 1, high, :],
            ref[n, p, real, :], ref[n, p + 2, real, :],
        )

    def flux(v, v_near, cc, c_near, left_w, right_w):
        total = left_w * (v - v_near[4]) + right_w * (v - v_near[5])
        for i in range(4):
            total = total + (cc + c_near[i]) * (v - v_near[i])
        return total

    def near_of(ref, n, slot, ghost, p):
        put_rows(ref, n, slot, p)
        v = ref[n, p + 1, real, :]
        return v, straight(ref, n, p) + sideways(v, ghost, p)

    def plane_loop(body, init):
        return lax.fori_loop(0, nz, body, init, unroll=2)

    blank = jnp.zeros((tx, width), jnp.float32)

    kappa_copy.wait()
    in_copy(0, 0).wait()
    for j in order[:3]:
        in_copy(0, j).wait_recv()
    time_send(0)
    for n in range(group):

        def body(p, packed):
            v = u[n + 1, p + 1, real, :]
            cc = kap[p] * (1.0 + v * v)
            c[n, p + 1, real, :] = cc
            slot = slots_state[n]
            return pack(slot, p, v, packed[0]), pack(slot + 1, p, cc, packed[1])

        packed = plane_loop(body, (blank, blank))
        col_send[slots_state[n]] = packed[0]
        col_send[slots_state[n] + 1] = packed[1]
        halo_send(slots_state[n], 2)

    half = 0.5 * tau_step
    for n in range(group):
        halo_wait(slots_state[n], 2)
        ghost_c = ghosts(slots_state[n] + 1)

        def body(p, carry):
            cc, c_near = near_of(c, n, slots_state[n] + 1, ghost_c, p)
            wl[n, p] = cc + c_near[4]
            wr[n, p] = cc + c_near[5]
            total = 6.0 * cc
            for item in c_near:
                total = total + item
            rd[n, p] = damping / (1.0 + half * total)
            return carry

        plane_loop(body, 0)

    in_copy(1, 0).wait()
    for j in order[:3]:
        in_copy(1, j).wait_recv()
    time_wait(0)
    for n in range(group):
        ghost_u = ghosts(slots_state[n])

        def body(p, packed):
            v, v_near = near_of(u, n + 1, slots_state[n], ghost_u, p)
            total = flux(v, v_near, c[n, p + 1, real, :], straight(c, n, p), wl[n, p], wr[n, p])
            left = src[n, p] - (v - u[n, p + 1, real, :] + half * total)
            res[n, p] = left
            update = left * rd[n, p]
            e1[n + 1, p + 1, real, :] = update
            return pack(slots_one[n], p, update, packed)

        col_send[slots_one[n]] = plane_loop(body, blank)
        halo_send(slots_one[n])
    time_send(1)

    for j in order:
        out_copy(0, j).start()

    time_wait(1)
    for n in range(group):
        halo_wait(slots_one[n])
        ghost = ghosts(slots_one[n])

        def body(p, packed):
            v, v_near = near_of(e1, n + 1, slots_one[n], ghost, p)
            total = flux(v, v_near, c[n, p + 1, real, :], straight(c, n, p), wl[n, p], wr[n, p])
            left = res[n, p] - (v - e1[n, p + 1, real, :] + half * total)
            update = v + left * rd[n, p]
            e2[n + 1, p + 1, real, :] = update
            return pack(slots_two[n], p, update, packed)

        col_send[slots_two[n]] = plane_loop(body, blank)
        halo_send(slots_two[n])
    time_send(2)

    def body(p, carry):
        for j in range(2):
            mc[j, p + 1] = 0.5 * (c[2 * j, p + 1] + c[2 * j + 1, p + 1])
            mwl[j, p] = 0.5 * (wl[2 * j, p] + wl[2 * j + 1, p])
            mwr[j, p] = 0.5 * (wr[2 * j, p] + wr[2 * j + 1, p])
        tc[0, p + 1] = 0.5 * (mc[0, p + 1] + mc[1, p + 1])
        return carry

    lax.fori_loop(0, nz, body, 0)

    def diagonal(ref, j, p, left_w, right_w, scale):
        cc = ref[j, p + 1, real, :]
        total = 4.0 * cc + left_w + right_w
        for item in straight(ref, j, p):
            total = total + item
        return damping / (1.0 + scale * total)

    time_wait(2)
    for j in range(2):
        halo_wait(slots_two[2 * j])
        halo_wait(slots_two[2 * j + 1])
        pair = [ghosts(slots_two[2 * j]), ghosts(slots_two[2 * j + 1])]

        def body(p, packed):
            rhs = None
            for i in range(2):
                n = 2 * j + i
                v, v_near = near_of(e2, n + 1, slots_two[n], pair[i], p)
                total = flux(
                    v, v_near, c[n, p + 1, real, :], straight(c, n, p), wl[n, p], wr[n, p]
                )
                left = res[n, p] - (v - e2[n, p + 1, real, :] + half * total)
                rhs = left if rhs is None else rhs + left
            inverse = diagonal(mc, j, p, mwl[j, p], mwr[j, p], 2.0 * half)
            mrd[j, p] = inverse
            mb[j, p] = rhs
            update = rhs * inverse
            me1[j + 1, p + 1, real, :] = update
            return pack(slots_mid_one[j], p, update, packed)

        col_send[slots_mid_one[j]] = plane_loop(body, blank)
        halo_send(slots_mid_one[j])
    time_send(3)

    time_wait(3)
    for j in range(2):
        halo_wait(slots_mid_one[j])
        ghost = ghosts(slots_mid_one[j])

        def body(p, packed):
            v, v_near = near_of(me1, j + 1, slots_mid_one[j], ghost, p)
            total = flux(v, v_near, mc[j, p + 1, real, :], straight(mc, j, p), mwl[j, p], mwr[j, p])
            left = mb[j, p] - (v - me1[j, p + 1, real, :] + 2.0 * half * total)
            update = v + left * mrd[j, p]
            me2[j + 1, p + 1, real, :] = update
            return pack(slots_mid_two[j], p, update, packed)

        col_send[slots_mid_two[j]] = plane_loop(body, blank)
        halo_send(slots_mid_two[j])
    time_send(4)

    time_wait(4)
    for j in range(2):
        halo_wait(slots_mid_two[j])
    pair = [ghosts(slots_mid_two[j]) for j in range(2)]

    def top_weights(p):
        return 0.5 * (mwl[0, p] + mwl[1, p]), 0.5 * (mwr[0, p] + mwr[1, p])

    def body(p, packed):
        rhs = None
        for j in range(2):
            v, v_near = near_of(me2, j + 1, slots_mid_two[j], pair[j], p)
            total = flux(v, v_near, mc[j, p + 1, real, :], straight(mc, j, p), mwl[j, p], mwr[j, p])
            left = mb[j, p] - (v - me2[j, p + 1, real, :] + 2.0 * half * total)
            rhs = left if rhs is None else rhs + left
        tb[p] = rhs
        update = rhs * diagonal(tc, 0, p, *top_weights(p), 4.0 * half)
        te[1, p + 1, real, :] = update
        return pack(slot_top, p, update, packed)

    col_send[slot_top] = plane_loop(body, blank)
    halo_send(slot_top)
    time_send(5)
    time_wait(5)
    halo_wait(slot_top)
    ghost = ghosts(slot_top)

    def body(p, carry):
        v, v_near = near_of(te, 1, slot_top, ghost, p)
        weights = top_weights(p)
        total = flux(v, v_near, tc[0, p + 1, real, :], straight(tc, 0, p), *weights)
        left = tb[p] - (v - te[0, p + 1, real, :] + 4.0 * half * total)
        update = v + left * diagonal(tc, 0, p, *weights, 4.0 * half)
        for n in range(group):
            mid = me2[n // 2 + 1, p + 1, real, :] + update
            new[n, p] = u[n + 1, p + 1, real, :] + (e2[n + 1, p + 1, real, :] + mid)
        return carry

    plane_loop(body, 0)
    for j in order:
        out_copy(1, j).start()

    for a in range(2):
        for j in order[:3]:
            in_copy(a, j).wait_send()
    for slot, count in [(slot, 2) for slot in slots_state] + [
        (slot, 1) for slot in range(slots_one[0], n_slots)
    ]:
        for number in range(4):

            @pl.when(sides[number][0])
            def _():
                halo_copy(slot, count, number).wait_send()

    if chained:

        @pl.when(has_next)
        def _():
            for number, (ref, last) in enumerate(time_refs):
                time_copy(number, ref, last).wait_send()

    for a in range(2):
        out_copy(a, 0).wait()
        for j in order[:3]:
            out_copy(a, j).wait_send()
            out_copy(a, j).wait_recv()


def shards(tm_size, space_size, iterate, source_term, conductivity):
    _, nz, tx, ty = conductivity.shape
    width = ty // group
    rows = tx + 2 * pad
    f32 = jnp.float32

    def padded(count):
        return pltpu.VMEM((count, nz + 2, rows, width), f32)

    def plain(*lead):
        return pltpu.VMEM((*lead, nz, tx, width), f32)

    dma = pltpu.SemaphoreType.DMA
    out = jax.ShapeDtypeStruct(iterate.shape, f32)
    hbm = pl.BlockSpec(memory_space=pl.ANY)
    return pl.pallas_call(
        functools.partial(kernel, tm_size, space_size),
        out_shape=(out, out),
        in_specs=[hbm] * 3,
        out_specs=(hbm, hbm),
        scratch_shapes=[
            padded(group + 1), padded(group), padded(group + 1), padded(group + 1),
            plain(), plain(group), plain(group), plain(group), plain(group), plain(group),
            padded(2), padded(3), padded(3), plain(2), plain(2), plain(2), plain(2),
            padded(1), padded(2), plain(), plain(group),
            pltpu.VMEM((2, n_slots, nz, width), f32), pltpu.VMEM((2, n_slots, nz, width), f32),
            pltpu.VMEM((n_slots, tx, width), f32), pltpu.VMEM((2, n_slots, tx, width), f32),
            dma((2, group - 1)), dma((2, group - 1)), dma((2, group - 1)), dma((2, group - 1)),
            dma((5,)), dma((4, n_slots)), dma((4, n_slots)), dma((6,)), dma((6,)),
        ],
        compiler_params=pltpu.CompilerParams(
            collective_id=0, has_side_effects=True, vmem_limit_bytes=48 * 2**20
        ),
    )(iterate, source_term, conductivity)


def solution(mesh):
    tiled = P("tm", "space", None, None, None)
    in_specs = (tiled, tiled, P("space", None, None, None))
    body = functools.partial(shards, mesh.shape["tm"], mesh.shape["space"])
    return jax.shard_map(
        body, mesh=mesh, in_specs=in_specs, out_specs=(tiled, tiled), check_vma=False
    )
```

```python
import functools

import jax
import jax.numpy as jnp
from jax import lax
from jax.experimental import pallas as pl
from jax.experimental.pallas import tpu as pltpu
from jax.sharding import PartitionSpec as P

tau_step = 0.08
damping = 0.7
group = 4
pad = 8
mesh_ids = pl.DeviceIdType.MESH

slots_state = [0, 2, 4, 6]
slots_one = [8, 9, 10, 11]
slots_two = [12, 13, 14, 15]
slots_mid_one = [16, 17]
slots_mid_two = [18, 19]
slot_top = 20
n_slots = 21
parts = 4
pace = {"one": 3, "two": 3, "mid_one": 2, "mid_two": 2, "top": 2}


def kernel(
    tm_size, space_size,
    state_in, source_in, kappa_in, new_out, res_out,
    u, c, e1, e2, kap, src, res, wl, wr, rd,
    mc, me1, me2, mb, mwl, mwr, mrd, tc, te, tb, new,
    row_send, row_recv, col_send, col_recv, own, beside, edge_send, edge_recv,
    in_ssem, in_rsem, out_ssem, out_rsem, out_lsem, e_ssem, e_rsem, loc_sem, h_ssem, h_rsem, t_ssem, t_rsem,
):
    nz, tx, width = kap.shape
    real = pl.ds(pad, tx)
    low = pl.ds(pad - 1, tx)
    high = pl.ds(pad + 1, tx)
    planes = pl.ds(1, nz)
    me = lax.axis_index("tm")
    sp = lax.axis_index("space")
    q = me % group
    base = me - q
    chained = tm_size > group
    has_dn, has_up = sp > 0, sp < space_size - 1
    has_left, has_right = q > 0, q < group - 1
    has_prev, has_next = base > 0, base + group < tm_size
    sides = [
        (has_dn, {"space": sp - 1}),
        (has_up, {"space": sp + 1}),
        (has_left, {"tm": me - 1}),
        (has_right, {"tm": me + 1}),
    ]

    def zero_edges(ref, count):
        for n in range(count):
            for plane in (0, nz + 1):
                ref[n, plane] = jnp.zeros(ref.shape[2:], jnp.float32)

    def columns(d):
        return pl.ds(pl.multiple_of(d * width, width), width)

    kappa_copy = pltpu.make_async_copy(kappa_in.at[0, :, :, columns(q)], kap, loc_sem.at[2])
    own_copy = pltpu.make_async_copy(state_in.at[0, 0], own, loc_sem.at[5])

    def beside_copy(side):
        block = kappa_in.at[0, :, :, columns(q - 1 + 2 * side)]
        return pltpu.make_async_copy(block, beside.at[side], loc_sem.at[6 + side])

    own_copy.start()
    kappa_copy.start()
    for side in range(2):

        @pl.when(sides[2 + side][0])
        def _():
            beside_copy(side).start()

    barrier = pltpu.get_barrier_semaphore()
    for j in range(1, group):
        pl.semaphore_signal(
            barrier, inc=1, device_id={"tm": base + (q + j) % group}, device_id_type=mesh_ids
        )
    greeted = [(has_dn, sides[0][1]), (has_up, sides[1][1])]
    if chained:
        greeted += [(has_prev, {"tm": me - group}), (has_next, {"tm": me + group})]
    for has, where in greeted:

        @pl.when(has)
        def _():
            pl.semaphore_signal(barrier, inc=1, device_id=where, device_id_type=mesh_ids)

    expected = group - 1
    for has, _ in greeted:
        expected = expected + jnp.where(has, 1, 0)
    pl.semaphore_wait(barrier, expected)

    def in_copy(a, j):
        d = (q + j) % group
        hbm = (state_in, source_in)[a].at[0, 0, :, :, columns(d)]
        dst = u.at[q + 1, planes, real, :] if a == 0 else src.at[q]
        if j == 0:
            return pltpu.make_async_copy(hbm, dst, loc_sem.at[a])
        return pltpu.make_async_remote_copy(
            src_ref=hbm, dst_ref=dst, send_sem=in_ssem.at[a, j - 1],
            recv_sem=in_rsem.at[a, j - 1], device_id={"tm": base + d}, device_id_type=mesh_ids,
        )

    def out_copy(a, j, part):
        d = (q + j) % group
        some = pl.ds(part * (nz // parts), nz // parts)
        hbm = (res_out, new_out)[a].at[0, 0, some, :, columns(q)]
        held = (res, new)[a].at[d, some]
        if j == 0:
            return pltpu.make_async_copy(held, hbm, out_lsem.at[a, part])
        return pltpu.make_async_remote_copy(
            src_ref=held, dst_ref=hbm, send_sem=out_ssem.at[a, part, j - 1],
            recv_sem=out_rsem.at[a, part, j - 1], device_id={"tm": base + d},
            device_id_type=mesh_ids,
        )

    order = (2, 1, 3, 0)
    for j in order:
        in_copy(0, j).start()

    zero_edges(u, group + 1)
    zero_edges(c, group)
    zero_edges(e1, group + 1)
    zero_edges(e2, group + 1)
    zero_edges(mc, 2)
    zero_edges(me1, 3)
    zero_edges(me2, 3)
    zero_edges(tc, 1)
    zero_edges(te, 2)

    @pl.when(jnp.logical_not(has_prev))
    def _():
        for ref in (u, e1, e2, me1, me2, te):
            ref[0] = jnp.zeros(ref.shape[1:], jnp.float32)

    for number, (has, _) in enumerate(sides):
        buffer = row_recv if number < 2 else col_recv

        @pl.when(jnp.logical_not(has))
        def _():
            buffer[number % 2] = jnp.zeros(buffer.shape[1:], jnp.float32)

    for side in range(2):

        @pl.when(jnp.logical_not(sides[2 + side][0]))
        def _():
            beside[side] = jnp.zeros(beside.shape[1:], jnp.float32)

    lane = lax.broadcasted_iota(jnp.int32, (tx, width), 1)
    blank = jnp.zeros((tx, width), jnp.float32)

    def pack_sides(p, left, right, packed):
        if left is not None:
            packed = jnp.where(lane == 2 * p + 1, pltpu.roll(left, 2 * p + 2, 1), packed)
        if right is not None:
            packed = jnp.where(lane == 2 * p, pltpu.roll(right, 2 * p, 1), packed)
        return packed

    def pack_body(p, packed):
        blocks = [own[p, :, d * width : (d + 1) * width] for d in range(group)]
        return tuple(
            pack_sides(
                p, blocks[d - 1] if d else None,
                blocks[d + 1] if d < group - 1 else None, packed[d],
            )
            for d in range(group)
        )

    own_copy.wait()
    packed = lax.fori_loop(0, nz, pack_body, (blank,) * group, unroll=4)
    for d in range(group):
        edge_send[d] = packed[d]
    edge_recv[q] = edge_send[q]

    def edge_copy(j):
        d = (q + j) % group
        return pltpu.make_async_remote_copy(
            src_ref=edge_send.at[d], dst_ref=edge_recv.at[q], send_sem=e_ssem.at[j - 1],
            recv_sem=e_rsem.at[j - 1], device_id={"tm": base + d}, device_id_type=mesh_ids,
        )

    for j in order[:3]:
        edge_copy(j).start()
    for j in order:
        in_copy(1, j).start()

    def halo_copy(slot, count, number):
        part = pl.ds(slot, count)
        opposite = number ^ 1
        if number < 2:
            source, target = row_send.at[number, part], row_recv.at[opposite, part]
        else:
            source, target = col_send.at[part], col_recv.at[opposite - 2, part]
        return pltpu.make_async_remote_copy(
            src_ref=source, dst_ref=target, send_sem=h_ssem.at[number, slot],
            recv_sem=h_rsem.at[opposite, slot], device_id=sides[number][1],
            device_id_type=mesh_ids,
        )

    def halo_send(slot, count=1, which=(2, 3, 0, 1)):
        for number in which:

            @pl.when(sides[number][0])
            def _():
                halo_copy(slot, count, number).start()

    def halo_wait(slot, count=1, which=(2, 3, 0, 1)):
        part = pl.ds(slot, count)
        for number in which:
            target = row_recv.at[number, part] if number < 2 else col_recv.at[number - 2, part]

            @pl.when(sides[number][0])
            def _():
                pltpu.make_async_remote_copy(
                    src_ref=target, dst_ref=target, send_sem=h_ssem.at[number, slot],
                    recv_sem=h_rsem.at[number, slot], device_id=sides[number][1],
                    device_id_type=mesh_ids,
                ).wait_recv()

    def time_copy(number, ref, last):
        return pltpu.make_async_remote_copy(
            src_ref=ref.at[last, planes, real, :], dst_ref=ref.at[0, planes, real, :],
            send_sem=t_ssem.at[number],
            recv_sem=t_rsem.at[number], device_id={"tm": me + group}, device_id_type=mesh_ids,
        )

    time_refs = [(u, group), (e1, group), (e2, group), (me1, 2), (me2, 2), (te, 1)]

    def time_send(number):
        if chained:

            @pl.when(has_next)
            def _():
                time_copy(number, *time_refs[number]).start()

    def time_wait(number):
        if chained:

            @pl.when(has_prev)
            def _():
                time_copy(number, *time_refs[number]).wait_recv()

    first_lane = lane == 0
    last_lane = lane == width - 1
    odd_lane = lane % 2 == 1
    pair_lane = lane // 2

    def put_send(slot, p, value):
        row_send[0, slot, pl.ds(p, 1), :] = value[:1]
        row_send[1, slot, pl.ds(p, 1), :] = value[tx - 1 :]

    def pack(slot, p, value, packed):
        put_send(slot, p, value)
        return jnp.where(pair_lane == p, pltpu.roll(value, 2 * p + 1, 1), packed)

    def ghosts(slot):
        return jnp.where(
            odd_lane,
            pltpu.roll(col_recv[0, slot], 1, 1),
            pltpu.roll(col_recv[1, slot], width - 1, 1),
        )

    def put_rows(ref, n, slot, p):
        ref[n, p + 1, pl.ds(pad - 1, 1), :] = row_recv[0, slot, pl.ds(p, 1), :]
        ref[n, p + 1, pl.ds(pad + tx, 1), :] = row_recv[1, slot, pl.ds(p, 1), :]

    def sideways(value, ghost, p):
        edge = pltpu.roll(ghost, width - 1 - 2 * p, 1)
        left = jnp.where(first_lane, edge, pltpu.roll(value, 1, 1))
        right = jnp.where(last_lane, edge, pltpu.roll(value, width - 1, 1))
        return left, right

    def straight(ref, n, p):
        return (
            ref[n, p + 1, low, :], ref[n, p + 1, high, :],
            ref[n, p, real, :], ref[n, p + 2, real, :],
        )

    def flux(v, v_near, cc, c_near, left_w, right_w):
        total = left_w * (v - v_near[4]) + right_w * (v - v_near[5])
        for i in range(4):
            total = total + (cc + c_near[i]) * (v - v_near[i])
        return total

    def near_of(ref, n, slot, ghost, p):
        put_rows(ref, n, slot, p)
        v = ref[n, p + 1, real, :]
        return v, straight(ref, n, p) + sideways(v, ghost, p)

    def plane_loop(body, init):
        return lax.fori_loop(0, nz, body, init, unroll=8)

    for side in range(2):

        @pl.when(sides[2 + side][0])
        def _():
            beside_copy(side).wait()

    def kappa_body(p, packed):
        return pack_sides(p, beside[0, p], beside[1, p], packed)

    kappa_edge = lax.fori_loop(0, nz, kappa_body, blank, unroll=4)

    kappa_copy.wait()
    in_copy(0, 0).wait()
    for j in order[:3]:
        in_copy(0, j).wait_recv()
    time_send(0)
    for n in range(group):

        def body(p, carry):
            v = u[n + 1, p + 1, real, :]
            cc = kap[p] * (1.0 + v * v)
            c[n, p + 1, real, :] = cc
            put_send(slots_state[n], p, v)
            put_send(slots_state[n] + 1, p, cc)
            return carry

        plane_loop(body, 0)
        halo_send(slots_state[n], 2, (0, 1))

    for j in order[:3]:
        edge_copy(j).wait_recv()
    half = 0.5 * tau_step
    for n in range(group):
        halo_wait(slots_state[n], 2, (0, 1))
        ghost_c = kappa_edge * (1.0 + edge_recv[n] * edge_recv[n])

        def body(p, carry):
            cc, c_near = near_of(c, n, slots_state[n] + 1, ghost_c, p)
            wl[n, p] = cc + c_near[4]
            wr[n, p] = cc + c_near[5]
            total = 6.0 * cc
            for item in c_near:
                total = total + item
            rd[n, p] = damping / (1.0 + half * total)
            return carry

        plane_loop(body, 0)

    in_copy(1, 0).wait()
    for j in order[:3]:
        in_copy(1, j).wait_recv()
    time_wait(0)
    for n in range(group):
        ghost_u = edge_recv[n]

        def body(p, packed):
            v, v_near = near_of(u, n + 1, slots_state[n], ghost_u, p)
            total = flux(v, v_near, c[n, p + 1, real, :], straight(c, n, p), wl[n, p], wr[n, p])
            left = src[n, p] - (v - u[n, p + 1, real, :] + half * total)
            res[n, p] = left
            update = left * rd[n, p]
            e1[n + 1, p + 1, real, :] = update
            return pack(slots_one[n], p, update, packed)

        col_send[slots_one[n]] = plane_loop(body, blank)
        halo_send(slots_one[n])
    time_send(1)

    pieces = [(j, part) for part in range(parts) for j in order]
    remote_pieces = [piece for piece in pieces if piece[0]]
    for part in range(parts):
        out_copy(0, 0, part).start()

    def give(stage):
        for _ in range(pace[stage]):
            out_copy(0, *remote_pieces.pop(0)).start()

    give("one")

    time_wait(1)
    for n in range(group):
        halo_wait(slots_one[n])
        ghost = ghosts(slots_one[n])

        def body(p, packed):
            v, v_near = near_of(e1, n + 1, slots_one[n], ghost, p)
            total = flux(v, v_near, c[n, p + 1, real, :], straight(c, n, p), wl[n, p], wr[n, p])
            left = res[n, p] - (v - e1[n, p + 1, real, :] + half * total)
            update = v + left * rd[n, p]
            e2[n + 1, p + 1, real, :] = update
            return pack(slots_two[n], p, update, packed)

        col_send[slots_two[n]] = plane_loop(body, blank)
        halo_send(slots_two[n])
    time_send(2)
    give("two")

    def body(p, carry):
        for j in range(2):
            mc[j, p + 1] = 0.5 * (c[2 * j, p + 1] + c[2 * j + 1, p + 1])
            mwl[j, p] = 0.5 * (wl[2 * j, p] + wl[2 * j + 1, p])
            mwr[j, p] = 0.5 * (wr[2 * j, p] + wr[2 * j + 1, p])
        tc[0, p + 1] = 0.5 * (mc[0, p + 1] + mc[1, p + 1])
        return carry

    lax.fori_loop(0, nz, body, 0)

    def diagonal(ref, j, p, left_w, right_w, scale):
        cc = ref[j, p + 1, real, :]
        total = 4.0 * cc + left_w + right_w
        for item in straight(ref, j, p):
            total = total + item
        return damping / (1.0 + scale * total)

    time_wait(2)
    for j in range(2):
        halo_wait(slots_two[2 * j])
        halo_wait(slots_two[2 * j + 1])
        pair = [ghosts(slots_two[2 * j]), ghosts(slots_two[2 * j + 1])]

        def body(p, packed):
            rhs = None
            for i in range(2):
                n = 2 * j + i
                v, v_near = near_of(e2, n + 1, slots_two[n], pair[i], p)
                total = flux(
                    v, v_near, c[n, p + 1, real, :], straight(c, n, p), wl[n, p], wr[n, p]
                )
                left = res[n, p] - (v - e2[n, p + 1, real, :] + half * total)
                rhs = left if rhs is None else rhs + left
            inverse = diagonal(mc, j, p, mwl[j, p], mwr[j, p], 2.0 * half)
            mrd[j, p] = inverse
            mb[j, p] = rhs
            update = rhs * inverse
            me1[j + 1, p + 1, real, :] = update
            return pack(slots_mid_one[j], p, update, packed)

        col_send[slots_mid_one[j]] = plane_loop(body, blank)
        halo_send(slots_mid_one[j])
    time_send(3)
    give("mid_one")

    time_wait(3)
    for j in range(2):
        halo_wait(slots_mid_one[j])
        ghost = ghosts(slots_mid_one[j])

        def body(p, packed):
            v, v_near = near_of(me1, j + 1, slots_mid_one[j], ghost, p)
            total = flux(v, v_near, mc[j, p + 1, real, :], straight(mc, j, p), mwl[j, p], mwr[j, p])
            left = mb[j, p] - (v - me1[j, p + 1, real, :] + 2.0 * half * total)
            update = v + left * mrd[j, p]
            me2[j + 1, p + 1, real, :] = update
            return pack(slots_mid_two[j], p, update, packed)

        col_send[slots_mid_two[j]] = plane_loop(body, blank)
        halo_send(slots_mid_two[j])
    time_send(4)
    give("mid_two")

    time_wait(4)
    for j in range(2):
        halo_wait(slots_mid_two[j])
    pair = [ghosts(slots_mid_two[j]) for j in range(2)]

    def top_weights(p):
        return 0.5 * (mwl[0, p] + mwl[1, p]), 0.5 * (mwr[0, p] + mwr[1, p])

    def body(p, packed):
        rhs = None
        for j in range(2):
            v, v_near = near_of(me2, j + 1, slots_mid_two[j], pair[j], p)
            total = flux(v, v_near, mc[j, p + 1, real, :], straight(mc, j, p), mwl[j, p], mwr[j, p])
            left = mb[j, p] - (v - me2[j, p + 1, real, :] + 2.0 * half * total)
            rhs = left if rhs is None else rhs + left
        tb[p] = rhs
        update = rhs * diagonal(tc, 0, p, *top_weights(p), 4.0 * half)
        te[1, p + 1, real, :] = update
        return pack(slot_top, p, update, packed)

    col_send[slot_top] = plane_loop(body, blank)
    halo_send(slot_top)
    time_send(5)
    give("top")
    time_wait(5)
    halo_wait(slot_top)
    ghost = ghosts(slot_top)

    def body(p, carry):
        v, v_near = near_of(te, 1, slot_top, ghost, p)
        weights = top_weights(p)
        total = flux(v, v_near, tc[0, p + 1, real, :], straight(tc, 0, p), *weights)
        left = tb[p] - (v - te[0, p + 1, real, :] + 4.0 * half * total)
        update = v + left * diagonal(tc, 0, p, *weights, 4.0 * half)
        for n in range(group):
            mid = me2[n // 2 + 1, p + 1, real, :] + update
            new[n, p] = u[n + 1, p + 1, real, :] + (e2[n + 1, p + 1, real, :] + mid)
        return carry

    for part in range(parts):
        first = part * (nz // parts)
        lax.fori_loop(first, first + nz // parts, body, 0, unroll=True)
        for j in order:
            out_copy(1, j, part).start()

    for j in order[:3]:
        edge_copy(j).wait_send()

    for a in range(2):
        for j in order[:3]:
            in_copy(a, j).wait_send()
    halos = [(slot, 2, (0, 1)) for slot in slots_state]
    halos += [(slot, 1, (0, 1, 2, 3)) for slot in range(slots_one[0], n_slots)]
    for slot, count, which in halos:
        for number in which:

            @pl.when(sides[number][0])
            def _():
                halo_copy(slot, count, number).wait_send()

    if chained:

        @pl.when(has_next)
        def _():
            for number, (ref, last) in enumerate(time_refs):
                time_copy(number, ref, last).wait_send()

    for a in range(2):
        for j, part in pieces:
            if j == 0:
                out_copy(a, j, part).wait()
            else:
                out_copy(a, j, part).wait_send()
                out_copy(a, j, part).wait_recv()


def shards(tm_size, space_size, iterate, source_term, conductivity):
    _, nz, tx, ty = conductivity.shape
    width = ty // group
    rows = tx + 2 * pad
    f32 = jnp.float32

    def padded(count):
        return pltpu.VMEM((count, nz + 2, rows, width), f32)

    def plain(*lead):
        return pltpu.VMEM((*lead, nz, tx, width), f32)

    dma = pltpu.SemaphoreType.DMA
    out = jax.ShapeDtypeStruct(iterate.shape, f32)
    hbm = pl.BlockSpec(memory_space=pltpu.HBM)
    return pl.pallas_call(
        functools.partial(kernel, tm_size, space_size),
        out_shape=(out, out),
        in_specs=[hbm] * 3,
        out_specs=(hbm, hbm),
        scratch_shapes=[
            padded(group + 1), padded(group), padded(group + 1), padded(group + 1),
            plain(), plain(group), plain(group), plain(group), plain(group), plain(group),
            padded(2), padded(3), padded(3), plain(2), plain(2), plain(2), plain(2),
            padded(1), padded(2), plain(), plain(group),
            pltpu.VMEM((2, n_slots, nz, width), f32), pltpu.VMEM((2, n_slots, nz, width), f32),
            pltpu.VMEM((n_slots, tx, width), f32), pltpu.VMEM((2, n_slots, tx, width), f32),
            pltpu.VMEM((nz, tx, ty), f32), plain(2),
            pltpu.VMEM((group, tx, width), f32), pltpu.VMEM((group, tx, width), f32),
            dma((2, group - 1)), dma((2, group - 1)),
            dma((2, parts, group - 1)), dma((2, parts, group - 1)), dma((2, parts)),
            dma((group - 1,)), dma((group - 1,)), dma((8,)), dma((4, n_slots)), dma((4, n_slots)), dma((6,)), dma((6,)),
        ],
        compiler_params=pltpu.CompilerParams(
            collective_id=0, has_side_effects=True, vmem_limit_bytes=48 * 2**20
        ),
    )(iterate, source_term, conductivity)


def solution(mesh):
    tiled = P("tm", "space", None, None, None)
    in_specs = (tiled, tiled, P("space", None, None, None))
    body = functools.partial(shards, mesh.shape["tm"], mesh.shape["space"])
    return jax.shard_map(
        body, mesh=mesh, in_specs=in_specs, out_specs=(tiled, tiled), check_vma=False
    )
```

```python
import functools

import jax
import jax.numpy as jnp
from jax import lax
from jax.experimental import pallas as pl
from jax.experimental.pallas import tpu as pltpu
from jax.sharding import PartitionSpec as P

tau_step = 0.08
damping = 0.7
group = 4
pad = 8
mesh_ids = pl.DeviceIdType.MESH

slots_state = [0, 2, 4, 6]
slots_one = [8, 9, 10, 11]
slots_two = [12, 13, 14, 15]
slots_mid_one = [16, 17]
slots_mid_two = [18, 19]
slot_top = 20
n_slots = 21
parts = 2
pace = {"one": 1, "two": 2, "mid_one": 1, "mid_two": 1, "top": 1}


def kernel(
    tm_size, space_size,
    state_in, source_in, kappa_in, new_out, res_out,
    u, c, e1, e2, kap, src, res, wl, wr, rd,
    mc, me1, me2, mb, mwl, mwr, mrd, tc, te, tb, new,
    row_send, row_recv, col_send, col_recv, own, beside, edge_send, edge_recv,
    in_ssem, in_rsem, out_ssem, out_rsem, out_lsem, in_lsem, e_ssem, e_rsem, loc_sem, h_ssem, h_rsem, t_ssem, t_rsem,
):
    nz, tx, width = kap.shape
    real = pl.ds(pad, tx)
    low = pl.ds(pad - 1, tx)
    high = pl.ds(pad + 1, tx)
    planes = pl.ds(1, nz)
    me = lax.axis_index("tm")
    sp = lax.axis_index("space")
    q = me % group
    base = me - q
    chained = tm_size > group
    has_dn, has_up = sp > 0, sp < space_size - 1
    has_left, has_right = q > 0, q < group - 1
    has_prev, has_next = base > 0, base + group < tm_size
    sides = [
        (has_dn, {"space": sp - 1}),
        (has_up, {"space": sp + 1}),
        (has_left, {"tm": me - 1}),
        (has_right, {"tm": me + 1}),
    ]

    def zero_edges(ref, count):
        for n in range(count):
            for plane in (0, nz + 1):
                ref[n, plane] = jnp.zeros(ref.shape[2:], jnp.float32)

    def columns(d):
        return pl.ds(pl.multiple_of(d * width, width), width)

    kappa_copy = pltpu.make_async_copy(kappa_in.at[0, :, :, columns(q)], kap, loc_sem.at[2])
    own_copy = pltpu.make_async_copy(state_in.at[0, 0], own, loc_sem.at[5])

    def beside_copy(side):
        block = kappa_in.at[0, :, :, columns(q - 1 + 2 * side)]
        return pltpu.make_async_copy(block, beside.at[side], loc_sem.at[6 + side])

    own_copy.start()
    kappa_copy.start()
    for side in range(2):

        @pl.when(sides[2 + side][0])
        def _():
            beside_copy(side).start()

    barrier = pltpu.get_barrier_semaphore()
    for j in range(1, group):
        pl.semaphore_signal(
            barrier, inc=1, device_id={"tm": base + (q + j) % group}, device_id_type=mesh_ids
        )
    greeted = [(has_dn, sides[0][1]), (has_up, sides[1][1])]
    if chained:
        greeted += [(has_prev, {"tm": me - group}), (has_next, {"tm": me + group})]
    for has, where in greeted:

        @pl.when(has)
        def _():
            pl.semaphore_signal(barrier, inc=1, device_id=where, device_id_type=mesh_ids)

    expected = group - 1
    for has, _ in greeted:
        expected = expected + jnp.where(has, 1, 0)
    pl.semaphore_wait(barrier, expected)

    def in_copy(a, j):
        d = (q + j) % group
        if a == 0:
            hbm, dst = state_in.at[0, 0, :, :, columns(d)], u.at[q + 1, planes, real, :]
        else:
            some = pl.ds((a - 1) * (nz // parts), nz // parts)
            hbm, dst = source_in.at[0, 0, some, :, columns(d)], src.at[q, some]
        if j == 0:
            return pltpu.make_async_copy(hbm, dst, in_lsem.at[a])
        return pltpu.make_async_remote_copy(
            src_ref=hbm, dst_ref=dst, send_sem=in_ssem.at[a, j - 1],
            recv_sem=in_rsem.at[a, j - 1], device_id={"tm": base + d}, device_id_type=mesh_ids,
        )

    def out_copy(a, j, part):
        d = (q + j) % group
        some = pl.ds(part * (nz // parts), nz // parts)
        hbm = (res_out, new_out)[a].at[0, 0, some, :, columns(q)]
        held = (res, new)[a].at[d, some]
        if j == 0:
            return pltpu.make_async_copy(held, hbm, out_lsem.at[a, part])
        return pltpu.make_async_remote_copy(
            src_ref=held, dst_ref=hbm, send_sem=out_ssem.at[a, part, j - 1],
            recv_sem=out_rsem.at[a, part, j - 1], device_id={"tm": base + d},
            device_id_type=mesh_ids,
        )

    order = (2, 1, 3, 0)
    for j in order:
        in_copy(0, j).start()

    zero_edges(u, group + 1)
    zero_edges(c, group)
    zero_edges(e1, group + 1)
    zero_edges(e2, group + 1)
    zero_edges(mc, 2)
    zero_edges(me1, 3)
    zero_edges(me2, 3)
    zero_edges(tc, 1)
    zero_edges(te, 2)

    @pl.when(jnp.logical_not(has_prev))
    def _():
        for ref in (u, e1, e2, me1, me2, te):
            ref[0] = jnp.zeros(ref.shape[1:], jnp.float32)

    for number, (has, _) in enumerate(sides):
        buffer = row_recv if number < 2 else col_recv

        @pl.when(jnp.logical_not(has))
        def _():
            buffer[number % 2] = jnp.zeros(buffer.shape[1:], jnp.float32)

    for side in range(2):

        @pl.when(jnp.logical_not(sides[2 + side][0]))
        def _():
            beside[side] = jnp.zeros(beside.shape[1:], jnp.float32)

    lane = lax.broadcasted_iota(jnp.int32, (tx, width), 1)
    blank = jnp.zeros((tx, width), jnp.float32)

    def pack_sides(p, left, right, packed):
        if left is not None:
            packed = jnp.where(lane == 2 * p + 1, pltpu.roll(left, 2 * p + 2, 1), packed)
        if right is not None:
            packed = jnp.where(lane == 2 * p, pltpu.roll(right, 2 * p, 1), packed)
        return packed

    def pack_body(p, packed):
        blocks = [own[p, :, d * width : (d + 1) * width] for d in range(group)]
        return tuple(
            pack_sides(
                p, blocks[d - 1] if d else None,
                blocks[d + 1] if d < group - 1 else None, packed[d],
            )
            for d in range(group)
        )

    own_copy.wait()
    packed = lax.fori_loop(0, nz, pack_body, (blank,) * group, unroll=4)
    for d in range(group):
        edge_send[d] = packed[d]
    edge_recv[q] = edge_send[q]

    def edge_copy(j):
        d = (q + j) % group
        return pltpu.make_async_remote_copy(
            src_ref=edge_send.at[d], dst_ref=edge_recv.at[q], send_sem=e_ssem.at[j - 1],
            recv_sem=e_rsem.at[j - 1], device_id={"tm": base + d}, device_id_type=mesh_ids,
        )

    for j in order[:3]:
        edge_copy(j).start()
    for part in range(parts):
        for j in order:
            in_copy(1 + part, j).start()

    def halo_copy(slot, count, number):
        part = pl.ds(slot, count)
        opposite = number ^ 1
        if number < 2:
            source, target = row_send.at[number, part], row_recv.at[opposite, part]
        else:
            source, target = col_send.at[part], col_recv.at[opposite - 2, part]
        return pltpu.make_async_remote_copy(
            src_ref=source, dst_ref=target, send_sem=h_ssem.at[number, slot],
            recv_sem=h_rsem.at[opposite, slot], device_id=sides[number][1],
            device_id_type=mesh_ids,
        )

    def halo_send(slot, count=1, which=(2, 3, 0, 1)):
        for number in which:

            @pl.when(sides[number][0])
            def _():
                halo_copy(slot, count, number).start()

    def halo_wait(slot, count=1, which=(2, 3, 0, 1)):
        part = pl.ds(slot, count)
        for number in which:
            target = row_recv.at[number, part] if number < 2 else col_recv.at[number - 2, part]

            @pl.when(sides[number][0])
            def _():
                pltpu.make_async_remote_copy(
                    src_ref=target, dst_ref=target, send_sem=h_ssem.at[number, slot],
                    recv_sem=h_rsem.at[number, slot], device_id=sides[number][1],
                    device_id_type=mesh_ids,
                ).wait_recv()

    def time_copy(number, ref, last):
        return pltpu.make_async_remote_copy(
            src_ref=ref.at[last, planes, real, :], dst_ref=ref.at[0, planes, real, :],
            send_sem=t_ssem.at[number],
            recv_sem=t_rsem.at[number], device_id={"tm": me + group}, device_id_type=mesh_ids,
        )

    time_refs = [(u, group), (e1, group), (e2, group), (me1, 2), (me2, 2), (te, 1)]

    def time_send(number):
        if chained:

            @pl.when(has_next)
            def _():
                time_copy(number, *time_refs[number]).start()

    def time_wait(number):
        if chained:

            @pl.when(has_prev)
            def _():
                time_copy(number, *time_refs[number]).wait_recv()

    first_lane = lane == 0
    last_lane = lane == width - 1
    odd_lane = lane % 2 == 1
    pair_lane = lane // 2

    def put_send(slot, p, value):
        row_send[0, slot, pl.ds(p, 1), :] = value[:1]
        row_send[1, slot, pl.ds(p, 1), :] = value[tx - 1 :]

    def pack(slot, p, value, packed):
        put_send(slot, p, value)
        return jnp.where(pair_lane == p, pltpu.roll(value, 2 * p + 1, 1), packed)

    def ghosts(slot):
        return jnp.where(
            odd_lane,
            pltpu.roll(col_recv[0, slot], 1, 1),
            pltpu.roll(col_recv[1, slot], width - 1, 1),
        )

    def put_rows(ref, n, slot, p):
        ref[n, p + 1, pl.ds(pad - 1, 1), :] = row_recv[0, slot, pl.ds(p, 1), :]
        ref[n, p + 1, pl.ds(pad + tx, 1), :] = row_recv[1, slot, pl.ds(p, 1), :]

    def sideways(value, ghost, p):
        edge = pltpu.roll(ghost, width - 1 - 2 * p, 1)
        left = jnp.where(first_lane, edge, pltpu.roll(value, 1, 1))
        right = jnp.where(last_lane, edge, pltpu.roll(value, width - 1, 1))
        return left, right

    def straight(ref, n, p):
        return (
            ref[n, p + 1, low, :], ref[n, p + 1, high, :],
            ref[n, p, real, :], ref[n, p + 2, real, :],
        )

    def flux(v, v_near, cc, c_near, left_w, right_w):
        total = left_w * (v - v_near[4]) + right_w * (v - v_near[5])
        for i in range(4):
            total = total + (cc + c_near[i]) * (v - v_near[i])
        return total

    def near_of(ref, n, slot, ghost, p):
        put_rows(ref, n, slot, p)
        v = ref[n, p + 1, real, :]
        return v, straight(ref, n, p) + sideways(v, ghost, p)

    def plane_loop(body, init):
        return lax.fori_loop(0, nz, body, init, unroll=8)

    for side in range(2):

        @pl.when(sides[2 + side][0])
        def _():
            beside_copy(side).wait()

    def kappa_body(p, packed):
        return pack_sides(p, beside[0, p], beside[1, p], packed)

    kappa_edge = lax.fori_loop(0, nz, kappa_body, blank, unroll=4)

    kappa_copy.wait()
    in_copy(0, 0).wait()
    for j in order[:3]:
        in_copy(0, j).wait_recv()
    time_send(0)
    for n in range(group):

        def body(p, carry):
            v = u[n + 1, p + 1, real, :]
            cc = kap[p] * (1.0 + v * v)
            c[n, p + 1, real, :] = cc
            put_send(slots_state[n], p, v)
            put_send(slots_state[n] + 1, p, cc)
            return carry

        plane_loop(body, 0)
        halo_send(slots_state[n], 2, (0, 1))

    time_wait(0)
    for j in order[:3]:
        edge_copy(j).wait_recv()
    half = 0.5 * tau_step
    for n in range(group):
        halo_wait(slots_state[n], 2, (0, 1))
        ghost_c = kappa_edge * (1.0 + edge_recv[n] * edge_recv[n])

        ghost_u = edge_recv[n]

        def body(p, carry):
            cc, c_near = near_of(c, n, slots_state[n] + 1, ghost_c, p)
            left_w, right_w = cc + c_near[4], cc + c_near[5]
            wl[n, p], wr[n, p] = left_w, right_w
            total = 6.0 * cc
            for item in c_near:
                total = total + item
            rd[n, p] = damping / (1.0 + half * total)
            v, v_near = near_of(u, n + 1, slots_state[n], ghost_u, p)
            total = flux(v, v_near, cc, c_near, left_w, right_w)
            res[n, p] = v - u[n, p + 1, real, :] + half * total
            return carry

        plane_loop(body, 0)

    for part in range(parts):
        in_copy(1 + part, 0).wait()
        for j in order[:3]:
            in_copy(1 + part, j).wait_recv()
        for n in range(group):

            def body(p, packed):
                left = src[n, p] - res[n, p]
                res[n, p] = left
                update = left * rd[n, p]
                e1[n + 1, p + 1, real, :] = update
                return pack(slots_one[n], p, update, packed)

            first = part * (nz // parts)
            packed = col_send[slots_one[n]] if part else blank
            col_send[slots_one[n]] = lax.fori_loop(
                first, first + nz // parts, body, packed, unroll=True
            )
            if part == parts - 1:
                halo_send(slots_one[n])
    time_send(1)

    pieces = [(j, part) for part in range(parts) for j in order]
    remote_pieces = [piece for piece in pieces if piece[0]]
    for part in range(parts):
        out_copy(0, 0, part).start()

    def give(stage):
        for _ in range(pace[stage]):
            out_copy(0, *remote_pieces.pop(0)).start()

    give("one")

    time_wait(1)
    for n in range(group):
        halo_wait(slots_one[n])
        ghost = ghosts(slots_one[n])

        def body(p, packed):
            v, v_near = near_of(e1, n + 1, slots_one[n], ghost, p)
            total = flux(v, v_near, c[n, p + 1, real, :], straight(c, n, p), wl[n, p], wr[n, p])
            left = res[n, p] - (v - e1[n, p + 1, real, :] + half * total)
            update = v + left * rd[n, p]
            e2[n + 1, p + 1, real, :] = update
            return pack(slots_two[n], p, update, packed)

        col_send[slots_two[n]] = plane_loop(body, blank)
        halo_send(slots_two[n])
    time_send(2)
    give("two")

    def body(p, carry):
        for j in range(2):
            mc[j, p + 1] = 0.5 * (c[2 * j, p + 1] + c[2 * j + 1, p + 1])
            mwl[j, p] = 0.5 * (wl[2 * j, p] + wl[2 * j + 1, p])
            mwr[j, p] = 0.5 * (wr[2 * j, p] + wr[2 * j + 1, p])
        tc[0, p + 1] = 0.5 * (mc[0, p + 1] + mc[1, p + 1])
        return carry

    lax.fori_loop(0, nz, body, 0)

    def diagonal(ref, j, p, left_w, right_w, scale):
        cc = ref[j, p + 1, real, :]
        total = 4.0 * cc + left_w + right_w
        for item in straight(ref, j, p):
            total = total + item
        return damping / (1.0 + scale * total)

    time_wait(2)
    for j in range(2):
        halo_wait(slots_two[2 * j])
        halo_wait(slots_two[2 * j + 1])
        pair = [ghosts(slots_two[2 * j]), ghosts(slots_two[2 * j + 1])]

        def body(p, packed):
            rhs = None
            for i in range(2):
                n = 2 * j + i
                v, v_near = near_of(e2, n + 1, slots_two[n], pair[i], p)
                total = flux(
                    v, v_near, c[n, p + 1, real, :], straight(c, n, p), wl[n, p], wr[n, p]
                )
                left = res[n, p] - (v - e2[n, p + 1, real, :] + half * total)
                rhs = left if rhs is None else rhs + left
            inverse = diagonal(mc, j, p, mwl[j, p], mwr[j, p], 2.0 * half)
            mrd[j, p] = inverse
            mb[j, p] = rhs
            update = rhs * inverse
            me1[j + 1, p + 1, real, :] = update
            return pack(slots_mid_one[j], p, update, packed)

        col_send[slots_mid_one[j]] = plane_loop(body, blank)
        halo_send(slots_mid_one[j])
    time_send(3)
    give("mid_one")

    time_wait(3)
    for j in range(2):
        halo_wait(slots_mid_one[j])
        ghost = ghosts(slots_mid_one[j])

        def body(p, packed):
            v, v_near = near_of(me1, j + 1, slots_mid_one[j], ghost, p)
            total = flux(v, v_near, mc[j, p + 1, real, :], straight(mc, j, p), mwl[j, p], mwr[j, p])
            left = mb[j, p] - (v - me1[j, p + 1, real, :] + 2.0 * half * total)
            update = v + left * mrd[j, p]
            me2[j + 1, p + 1, real, :] = update
            return pack(slots_mid_two[j], p, update, packed)

        col_send[slots_mid_two[j]] = plane_loop(body, blank)
        halo_send(slots_mid_two[j])
    time_send(4)
    give("mid_two")

    time_wait(4)
    for j in range(2):
        halo_wait(slots_mid_two[j])
    pair = [ghosts(slots_mid_two[j]) for j in range(2)]

    def top_weights(p):
        return 0.5 * (mwl[0, p] + mwl[1, p]), 0.5 * (mwr[0, p] + mwr[1, p])

    def body(p, packed):
        rhs = None
        for j in range(2):
            v, v_near = near_of(me2, j + 1, slots_mid_two[j], pair[j], p)
            total = flux(v, v_near, mc[j, p + 1, real, :], straight(mc, j, p), mwl[j, p], mwr[j, p])
            left = mb[j, p] - (v - me2[j, p + 1, real, :] + 2.0 * half * total)
            rhs = left if rhs is None else rhs + left
        tb[p] = rhs
        update = rhs * diagonal(tc, 0, p, *top_weights(p), 4.0 * half)
        te[1, p + 1, real, :] = update
        return pack(slot_top, p, update, packed)

    col_send[slot_top] = plane_loop(body, blank)
    halo_send(slot_top)
    time_send(5)
    give("top")
    time_wait(5)
    halo_wait(slot_top)
    ghost = ghosts(slot_top)

    def body(p, carry):
        v, v_near = near_of(te, 1, slot_top, ghost, p)
        weights = top_weights(p)
        total = flux(v, v_near, tc[0, p + 1, real, :], straight(tc, 0, p), *weights)
        left = tb[p] - (v - te[0, p + 1, real, :] + 4.0 * half * total)
        update = v + left * diagonal(tc, 0, p, *weights, 4.0 * half)
        for n in range(group):
            mid = me2[n // 2 + 1, p + 1, real, :] + update
            new[n, p] = u[n + 1, p + 1, real, :] + (e2[n + 1, p + 1, real, :] + mid)
        return carry

    for part in range(parts):
        first = part * (nz // parts)
        lax.fori_loop(first, first + nz // parts, body, 0, unroll=True)
        for j in order:
            out_copy(1, j, part).start()

    for j in order[:3]:
        edge_copy(j).wait_send()

    for a in range(1 + parts):
        for j in order[:3]:
            in_copy(a, j).wait_send()
    halos = [(slot, 2, (0, 1)) for slot in slots_state]
    halos += [(slot, 1, (0, 1, 2, 3)) for slot in range(slots_one[0], n_slots)]
    for slot, count, which in halos:
        for number in which:

            @pl.when(sides[number][0])
            def _():
                halo_copy(slot, count, number).wait_send()

    if chained:

        @pl.when(has_next)
        def _():
            for number, (ref, last) in enumerate(time_refs):
                time_copy(number, ref, last).wait_send()

    for a in range(2):
        for j, part in pieces:
            if j == 0:
                out_copy(a, j, part).wait()
            else:
                out_copy(a, j, part).wait_send()
                out_copy(a, j, part).wait_recv()


def shards(tm_size, space_size, iterate, source_term, conductivity):
    _, nz, tx, ty = conductivity.shape
    width = ty // group
    rows = tx + 2 * pad
    f32 = jnp.float32

    def padded(count):
        return pltpu.VMEM((count, nz + 2, rows, width), f32)

    def plain(*lead):
        return pltpu.VMEM((*lead, nz, tx, width), f32)

    dma = pltpu.SemaphoreType.DMA
    out = jax.ShapeDtypeStruct(iterate.shape, f32)
    hbm = pl.BlockSpec(memory_space=pltpu.HBM)
    return pl.pallas_call(
        functools.partial(kernel, tm_size, space_size),
        out_shape=(out, out),
        in_specs=[hbm] * 3,
        out_specs=(hbm, hbm),
        scratch_shapes=[
            padded(group + 1), padded(group), padded(group + 1), padded(group + 1),
            plain(), plain(group), plain(group), plain(group), plain(group), plain(group),
            padded(2), padded(3), padded(3), plain(2), plain(2), plain(2), plain(2),
            padded(1), padded(2), plain(), plain(group),
            pltpu.VMEM((2, n_slots, nz, width), f32), pltpu.VMEM((2, n_slots, nz, width), f32),
            pltpu.VMEM((n_slots, tx, width), f32), pltpu.VMEM((2, n_slots, tx, width), f32),
            pltpu.VMEM((nz, tx, ty), f32), plain(2),
            pltpu.VMEM((group, tx, width), f32), pltpu.VMEM((group, tx, width), f32),
            dma((1 + parts, group - 1)), dma((1 + parts, group - 1)),
            dma((2, parts, group - 1)), dma((2, parts, group - 1)), dma((2, parts)), dma((1 + parts,)),
            dma((group - 1,)), dma((group - 1,)), dma((8,)), dma((4, n_slots)), dma((4, n_slots)), dma((6,)), dma((6,)),
        ],
        compiler_params=pltpu.CompilerParams(
            collective_id=0, has_side_effects=True, vmem_limit_bytes=67043328
        ),
    )(iterate, source_term, conductivity)


def solution(mesh):
    tiled = P("tm", "space", None, None, None)
    in_specs = (tiled, tiled, P("space", None, None, None))
    body = functools.partial(shards, mesh.shape["tm"], mesh.shape["space"])
    return jax.shard_map(
        body, mesh=mesh, in_specs=in_specs, out_specs=(tiled, tiled), check_vma=False
    )
```

```python
import functools

import jax
import jax.numpy as jnp
from jax import lax
from jax.experimental import pallas as pl
from jax.experimental.pallas import tpu as pltpu
from jax.sharding import PartitionSpec as P

tau_step = 0.08
damping = 0.7
group = 4
pad = 8
mesh_ids = pl.DeviceIdType.MESH

slots_state = [0, 2, 4, 6]
slots_one = [8, 9, 10, 11]
slots_two = [12, 13, 14, 15]
slots_mid_one = [16, 17]
slots_mid_two = [18, 19]
slot_top = 20
n_slots = 21
parts = 2
pace = {"one": 2, "two": 1, "mid_one": 1, "mid_two": 1, "top": 1}


def kernel(
    tm_size, space_size,
    state_in, source_in, kappa_in, new_out, res_out,
    u, c, e1, e2, kap, src, res, wl, wr, rd,
    mc, me1, me2, mb, mwl, mwr, mrd, tc, te, tb, new,
    row_send, row_recv, col_send, col_recv, own, beside, edge_send, edge_recv,
    in_ssem, in_rsem, out_ssem, out_rsem, out_lsem, in_lsem, e_ssem, e_rsem, loc_sem, h_ssem, h_rsem, t_ssem, t_rsem,
):
    nz, tx, width = kap.shape
    real = pl.ds(pad, tx)
    low = pl.ds(pad - 1, tx)
    high = pl.ds(pad + 1, tx)
    planes = pl.ds(1, nz)
    me = lax.axis_index("tm")
    sp = lax.axis_index("space")
    q = me % group
    base = me - q
    chained = tm_size > group
    has_dn, has_up = sp > 0, sp < space_size - 1
    has_left, has_right = q > 0, q < group - 1
    has_prev, has_next = base > 0, base + group < tm_size
    sides = [
        (has_dn, {"space": sp - 1}),
        (has_up, {"space": sp + 1}),
        (has_left, {"tm": me - 1}),
        (has_right, {"tm": me + 1}),
    ]

    def zero_edges(ref, count):
        for n in range(count):
            for plane in (0, nz + 1):
                ref[n, plane] = jnp.zeros(ref.shape[2:], jnp.float32)

    def columns(d):
        return pl.ds(pl.multiple_of(d * width, width), width)

    kappa_copy = pltpu.make_async_copy(kappa_in.at[0, :, :, columns(q)], kap, loc_sem.at[2])
    own_copy = pltpu.make_async_copy(state_in.at[0, 0], own, loc_sem.at[5])

    def beside_copy(side):
        block = kappa_in.at[0, :, :, columns(q - 1 + 2 * side)]
        return pltpu.make_async_copy(block, beside.at[side], loc_sem.at[6 + side])

    own_copy.start()
    kappa_copy.start()
    for side in range(2):

        @pl.when(sides[2 + side][0])
        def _():
            beside_copy(side).start()

    barrier = pltpu.get_barrier_semaphore()
    for j in range(1, group):
        pl.semaphore_signal(
            barrier, inc=1, device_id={"tm": base + (q + j) % group}, device_id_type=mesh_ids
        )
    greeted = [(has_dn, sides[0][1]), (has_up, sides[1][1])]
    if chained:
        greeted += [(has_prev, {"tm": me - group}), (has_next, {"tm": me + group})]
    for has, where in greeted:

        @pl.when(has)
        def _():
            pl.semaphore_signal(barrier, inc=1, device_id=where, device_id_type=mesh_ids)

    expected = group - 1
    for has, _ in greeted:
        expected = expected + jnp.where(has, 1, 0)
    pl.semaphore_wait(barrier, expected)

    def in_copy(a, j):
        d = (q + j) % group
        if a == 0:
            hbm, dst = state_in.at[0, 0, :, :, columns(d)], u.at[q + 1, planes, real, :]
        else:
            some = pl.ds((a - 1) * (nz // parts), nz // parts)
            hbm, dst = source_in.at[0, 0, some, :, columns(d)], src.at[q, some]
        if j == 0:
            return pltpu.make_async_copy(hbm, dst, in_lsem.at[a])
        return pltpu.make_async_remote_copy(
            src_ref=hbm, dst_ref=dst, send_sem=in_ssem.at[a, j - 1],
            recv_sem=in_rsem.at[a, j - 1], device_id={"tm": base + d}, device_id_type=mesh_ids,
        )

    def out_copy(a, j, part):
        d = (q + j) % group
        some = pl.ds(part * (nz // parts), nz // parts)
        hbm = (res_out, new_out)[a].at[0, 0, some, :, columns(q)]
        held = (res, new)[a].at[d, some]
        if j == 0:
            return pltpu.make_async_copy(held, hbm, out_lsem.at[a, part])
        return pltpu.make_async_remote_copy(
            src_ref=held, dst_ref=hbm, send_sem=out_ssem.at[a, part, j - 1],
            recv_sem=out_rsem.at[a, part, j - 1], device_id={"tm": base + d},
            device_id_type=mesh_ids,
        )

    order = (2, 1, 3, 0)
    for j in order:
        in_copy(0, j).start()

    zero_edges(u, group + 1)
    zero_edges(c, group)
    zero_edges(e1, group + 1)
    zero_edges(e2, group + 1)
    zero_edges(mc, 2)
    zero_edges(me1, 3)
    zero_edges(me2, 3)
    zero_edges(tc, 1)
    zero_edges(te, 2)

    @pl.when(jnp.logical_not(has_prev))
    def _():
        for ref in (u, e1, e2, me1, me2, te):
            ref[0] = jnp.zeros(ref.shape[1:], jnp.float32)

    for number, (has, _) in enumerate(sides):
        buffer = row_recv if number < 2 else col_recv

        @pl.when(jnp.logical_not(has))
        def _():
            buffer[number % 2] = jnp.zeros(buffer.shape[1:], jnp.float32)

    for side in range(2):

        @pl.when(jnp.logical_not(sides[2 + side][0]))
        def _():
            beside[side] = jnp.zeros(beside.shape[1:], jnp.float32)

    lane = lax.broadcasted_iota(jnp.int32, (tx, width), 1)
    blank = jnp.zeros((tx, width), jnp.float32)

    def pack_sides(p, left, right, packed):
        if left is not None:
            packed = jnp.where(lane == 2 * p + 1, pltpu.roll(left, 2 * p + 2, 1), packed)
        if right is not None:
            packed = jnp.where(lane == 2 * p, pltpu.roll(right, 2 * p, 1), packed)
        return packed

    def pack_body(p, packed):
        blocks = [own[p, :, d * width : (d + 1) * width] for d in range(group)]
        return tuple(
            pack_sides(
                p, blocks[d - 1] if d else None,
                blocks[d + 1] if d < group - 1 else None, packed[d],
            )
            for d in range(group)
        )

    own_copy.wait()
    packed = lax.fori_loop(0, nz, pack_body, (blank,) * group, unroll=4)
    for d in range(group):
        edge_send[d] = packed[d]
    edge_recv[q] = edge_send[q]

    def edge_copy(j):
        d = (q + j) % group
        return pltpu.make_async_remote_copy(
            src_ref=edge_send.at[d], dst_ref=edge_recv.at[q], send_sem=e_ssem.at[j - 1],
            recv_sem=e_rsem.at[j - 1], device_id={"tm": base + d}, device_id_type=mesh_ids,
        )

    for j in order[:3]:
        edge_copy(j).start()
    for part in range(parts):
        for j in order:
            in_copy(1 + part, j).start()

    def halo_copy(slot, count, number):
        part = pl.ds(slot, count)
        opposite = number ^ 1
        if number < 2:
            source, target = row_send.at[number, part], row_recv.at[opposite, part]
        else:
            source, target = col_send.at[part], col_recv.at[opposite - 2, part]
        return pltpu.make_async_remote_copy(
            src_ref=source, dst_ref=target, send_sem=h_ssem.at[number, slot],
            recv_sem=h_rsem.at[opposite, slot], device_id=sides[number][1],
            device_id_type=mesh_ids,
        )

    def halo_send(slot, count=1, which=(2, 3, 0, 1)):
        for number in which:

            @pl.when(sides[number][0])
            def _():
                halo_copy(slot, count, number).start()

    def halo_wait(slot, count=1, which=(2, 3, 0, 1)):
        part = pl.ds(slot, count)
        for number in which:
            target = row_recv.at[number, part] if number < 2 else col_recv.at[number - 2, part]

            @pl.when(sides[number][0])
            def _():
                pltpu.make_async_remote_copy(
                    src_ref=target, dst_ref=target, send_sem=h_ssem.at[number, slot],
                    recv_sem=h_rsem.at[number, slot], device_id=sides[number][1],
                    device_id_type=mesh_ids,
                ).wait_recv()

    def time_copy(number, ref, last):
        return pltpu.make_async_remote_copy(
            src_ref=ref.at[last, planes, real, :], dst_ref=ref.at[0, planes, real, :],
            send_sem=t_ssem.at[number],
            recv_sem=t_rsem.at[number], device_id={"tm": me + group}, device_id_type=mesh_ids,
        )

    time_refs = [(u, group), (e1, group), (e2, group), (me1, 2), (me2, 2), (te, 1)]

    def time_send(number):
        if chained:

            @pl.when(has_next)
            def _():
                time_copy(number, *time_refs[number]).start()

    def time_wait(number):
        if chained:

            @pl.when(has_prev)
            def _():
                time_copy(number, *time_refs[number]).wait_recv()

    first_lane = lane == 0
    last_lane = lane == width - 1
    odd_lane = lane % 2 == 1
    pair_lane = lane // 2

    def put_send(slot, p, value):
        row_send[0, slot, pl.ds(p, 1), :] = value[:1]
        row_send[1, slot, pl.ds(p, 1), :] = value[tx - 1 :]

    def pack(slot, p, value, packed):
        put_send(slot, p, value)
        return jnp.where(pair_lane == p, pltpu.roll(value, 2 * p + 1, 1), packed)

    def ghosts(slot):
        return jnp.where(
            odd_lane,
            pltpu.roll(col_recv[0, slot], 1, 1),
            pltpu.roll(col_recv[1, slot], width - 1, 1),
        )

    def put_rows(ref, n, slot, p):
        ref[n, p + 1, pl.ds(pad - 1, 1), :] = row_recv[0, slot, pl.ds(p, 1), :]
        ref[n, p + 1, pl.ds(pad + tx, 1), :] = row_recv[1, slot, pl.ds(p, 1), :]

    def sideways(value, ghost, p):
        edge = pltpu.roll(ghost, width - 1 - 2 * p, 1)
        left = jnp.where(first_lane, edge, pltpu.roll(value, 1, 1))
        right = jnp.where(last_lane, edge, pltpu.roll(value, width - 1, 1))
        return left, right

    def straight(ref, n, p):
        return (
            ref[n, p + 1, low, :], ref[n, p + 1, high, :],
            ref[n, p, real, :], ref[n, p + 2, real, :],
        )

    def flux(v, v_near, cc, c_near, left_w, right_w):
        total = left_w * (v - v_near[4]) + right_w * (v - v_near[5])
        for i in range(4):
            total = total + (cc + c_near[i]) * (v - v_near[i])
        return total

    def near_of(ref, n, slot, ghost, p):
        put_rows(ref, n, slot, p)
        v = ref[n, p + 1, real, :]
        return v, straight(ref, n, p) + sideways(v, ghost, p)

    def plane_loop(body, init):
        return lax.fori_loop(0, nz, body, init, unroll=8)

    for side in range(2):

        @pl.when(sides[2 + side][0])
        def _():
            beside_copy(side).wait()

    def kappa_body(p, packed):
        return pack_sides(p, beside[0, p], beside[1, p], packed)

    kappa_edge = lax.fori_loop(0, nz, kappa_body, blank, unroll=4)

    kappa_copy.wait()
    in_copy(0, 0).wait()
    for j in order[:3]:
        in_copy(0, j).wait_recv()
    time_send(0)
    for n in range(group):

        def body(p, carry):
            v = u[n + 1, p + 1, real, :]
            cc = kap[p] * (1.0 + v * v)
            c[n, p + 1, real, :] = cc
            put_send(slots_state[n], p, v)
            put_send(slots_state[n] + 1, p, cc)
            return carry

        plane_loop(body, 0)
        halo_send(slots_state[n], 2, (0, 1))

    time_wait(0)
    for j in order[:3]:
        edge_copy(j).wait_recv()
    half = 0.5 * tau_step
    for n in range(group):
        halo_wait(slots_state[n], 2, (0, 1))
        ghost_c = kappa_edge * (1.0 + edge_recv[n] * edge_recv[n])

        ghost_u = edge_recv[n]

        def body(p, carry):
            cc, c_near = near_of(c, n, slots_state[n] + 1, ghost_c, p)
            left_w, right_w = cc + c_near[4], cc + c_near[5]
            wl[n, p], wr[n, p] = left_w, right_w
            total = 6.0 * cc
            for item in c_near:
                total = total + item
            rd[n, p] = damping / (1.0 + half * total)
            v, v_near = near_of(u, n + 1, slots_state[n], ghost_u, p)
            total = flux(v, v_near, cc, c_near, left_w, right_w)
            res[n, p] = v - u[n, p + 1, real, :] + half * total
            return carry

        plane_loop(body, 0)

    for part in range(parts):
        in_copy(1 + part, 0).wait()
        for j in order[:3]:
            in_copy(1 + part, j).wait_recv()
        for n in range(group):

            def body(p, packed):
                left = src[n, p] - res[n, p]
                res[n, p] = left
                update = left * rd[n, p]
                e1[n + 1, p + 1, real, :] = update
                return pack(slots_one[n], p, update, packed)

            first = part * (nz // parts)
            packed = col_send[slots_one[n]] if part else blank
            col_send[slots_one[n]] = lax.fori_loop(
                first, first + nz // parts, body, packed, unroll=True
            )
            if part == parts - 1:
                halo_send(slots_one[n])
    time_send(1)

    pieces = [(j, part) for part in range(parts) for j in order]
    remote_pieces = [piece for piece in pieces if piece[0]]
    for part in range(parts):
        out_copy(0, 0, part).start()

    def give(stage):
        for _ in range(pace[stage]):
            out_copy(0, *remote_pieces.pop(0)).start()

    give("one")

    time_wait(1)
    for n in range(group):
        halo_wait(slots_one[n])
        ghost = ghosts(slots_one[n])

        def body(p, packed):
            v, v_near = near_of(e1, n + 1, slots_one[n], ghost, p)
            total = flux(v, v_near, c[n, p + 1, real, :], straight(c, n, p), wl[n, p], wr[n, p])
            left = res[n, p] - (v - e1[n, p + 1, real, :] + half * total)
            update = v + left * rd[n, p]
            e2[n + 1, p + 1, real, :] = update
            return pack(slots_two[n], p, update, packed)

        col_send[slots_two[n]] = plane_loop(body, blank)
        halo_send(slots_two[n])
    time_send(2)
    give("two")

    def body(p, carry):
        for j in range(2):
            mc[j, p + 1] = 0.5 * (c[2 * j, p + 1] + c[2 * j + 1, p + 1])
            mwl[j, p] = 0.5 * (wl[2 * j, p] + wl[2 * j + 1, p])
            mwr[j, p] = 0.5 * (wr[2 * j, p] + wr[2 * j + 1, p])
        tc[0, p + 1] = 0.5 * (mc[0, p + 1] + mc[1, p + 1])
        return carry

    lax.fori_loop(0, nz, body, 0)

    def diagonal(ref, j, p, left_w, right_w, scale):
        cc = ref[j, p + 1, real, :]
        total = 4.0 * cc + left_w + right_w
        for item in straight(ref, j, p):
            total = total + item
        return damping / (1.0 + scale * total)

    time_wait(2)
    for j in range(2):
        halo_wait(slots_two[2 * j])
        halo_wait(slots_two[2 * j + 1])
        pair = [ghosts(slots_two[2 * j]), ghosts(slots_two[2 * j + 1])]

        def body(p, packed):
            rhs = None
            for i in range(2):
                n = 2 * j + i
                v, v_near = near_of(e2, n + 1, slots_two[n], pair[i], p)
                total = flux(
                    v, v_near, c[n, p + 1, real, :], straight(c, n, p), wl[n, p], wr[n, p]
                )
                left = res[n, p] - (v - e2[n, p + 1, real, :] + half * total)
                rhs = left if rhs is None else rhs + left
            inverse = diagonal(mc, j, p, mwl[j, p], mwr[j, p], 2.0 * half)
            mrd[j, p] = inverse
            mb[j, p] = rhs
            update = rhs * inverse
            me1[j + 1, p + 1, real, :] = update
            return pack(slots_mid_one[j], p, update, packed)

        col_send[slots_mid_one[j]] = plane_loop(body, blank)
        halo_send(slots_mid_one[j])
    time_send(3)
    give("mid_one")

    time_wait(3)
    for j in range(2):
        halo_wait(slots_mid_one[j])
        ghost = ghosts(slots_mid_one[j])

        def body(p, packed):
            v, v_near = near_of(me1, j + 1, slots_mid_one[j], ghost, p)
            total = flux(v, v_near, mc[j, p + 1, real, :], straight(mc, j, p), mwl[j, p], mwr[j, p])
            left = mb[j, p] - (v - me1[j, p + 1, real, :] + 2.0 * half * total)
            update = v + left * mrd[j, p]
            me2[j + 1, p + 1, real, :] = update
            return pack(slots_mid_two[j], p, update, packed)

        col_send[slots_mid_two[j]] = plane_loop(body, blank)
        halo_send(slots_mid_two[j])
    time_send(4)
    give("mid_two")

    time_wait(4)
    for j in range(2):
        halo_wait(slots_mid_two[j])
    pair = [ghosts(slots_mid_two[j]) for j in range(2)]

    def top_weights(p):
        return 0.5 * (mwl[0, p] + mwl[1, p]), 0.5 * (mwr[0, p] + mwr[1, p])

    def body(p, packed):
        rhs = None
        for j in range(2):
            v, v_near = near_of(me2, j + 1, slots_mid_two[j], pair[j], p)
            total = flux(v, v_near, mc[j, p + 1, real, :], straight(mc, j, p), mwl[j, p], mwr[j, p])
            left = mb[j, p] - (v - me2[j, p + 1, real, :] + 2.0 * half * total)
            rhs = left if rhs is None else rhs + left
        tb[p] = rhs
        update = rhs * diagonal(tc, 0, p, *top_weights(p), 4.0 * half)
        te[1, p + 1, real, :] = update
        return pack(slot_top, p, update, packed)

    col_send[slot_top] = plane_loop(body, blank)
    halo_send(slot_top)
    time_send(5)
    give("top")
    time_wait(5)
    halo_wait(slot_top)
    ghost = ghosts(slot_top)

    def body(p, carry):
        v, v_near = near_of(te, 1, slot_top, ghost, p)
        weights = top_weights(p)
        total = flux(v, v_near, tc[0, p + 1, real, :], straight(tc, 0, p), *weights)
        left = tb[p] - (v - te[0, p + 1, real, :] + 4.0 * half * total)
        update = v + left * diagonal(tc, 0, p, *weights, 4.0 * half)
        for n in range(group):
            mid = me2[n // 2 + 1, p + 1, real, :] + update
            new[n, p] = u[n + 1, p + 1, real, :] + (e2[n + 1, p + 1, real, :] + mid)
        return carry

    for part in range(parts):
        first = part * (nz // parts)
        lax.fori_loop(first, first + nz // parts, body, 0, unroll=True)
        for j in order:
            out_copy(1, j, part).start()

    for j in order[:3]:
        edge_copy(j).wait_send()

    for a in range(1 + parts):
        for j in order[:3]:
            in_copy(a, j).wait_send()
    halos = [(slot, 2, (0, 1)) for slot in slots_state]
    halos += [(slot, 1, (0, 1, 2, 3)) for slot in range(slots_one[0], n_slots)]
    for slot, count, which in halos:
        for number in which:

            @pl.when(sides[number][0])
            def _():
                halo_copy(slot, count, number).wait_send()

    if chained:

        @pl.when(has_next)
        def _():
            for number, (ref, last) in enumerate(time_refs):
                time_copy(number, ref, last).wait_send()

    for a in range(2):
        for j, part in pieces:
            if j == 0:
                out_copy(a, j, part).wait()
            else:
                out_copy(a, j, part).wait_send()
                out_copy(a, j, part).wait_recv()


def shards(tm_size, space_size, iterate, source_term, conductivity):
    _, nz, tx, ty = conductivity.shape
    width = ty // group
    rows = tx + 2 * pad
    f32 = jnp.float32

    def padded(count):
        return pltpu.VMEM((count, nz + 2, rows, width), f32)

    def plain(*lead):
        return pltpu.VMEM((*lead, nz, tx, width), f32)

    dma = pltpu.SemaphoreType.DMA
    out = jax.ShapeDtypeStruct(iterate.shape, f32)
    hbm = pl.BlockSpec(memory_space=pltpu.HBM)
    return pl.pallas_call(
        functools.partial(kernel, tm_size, space_size),
        out_shape=(out, out),
        in_specs=[hbm] * 3,
        out_specs=(hbm, hbm),
        scratch_shapes=[
            padded(group + 1), padded(group), padded(group + 1), padded(group + 1),
            plain(), plain(group), plain(group), plain(group), plain(group), plain(group),
            padded(2), padded(3), padded(3), plain(2), plain(2), plain(2), plain(2),
            padded(1), padded(2), plain(), plain(group),
            pltpu.VMEM((2, n_slots, nz, width), f32), pltpu.VMEM((2, n_slots, nz, width), f32),
            pltpu.VMEM((n_slots, tx, width), f32), pltpu.VMEM((2, n_slots, tx, width), f32),
            pltpu.VMEM((nz, tx, ty), f32), plain(2),
            pltpu.VMEM((group, tx, width), f32), pltpu.VMEM((group, tx, width), f32),
            dma((1 + parts, group - 1)), dma((1 + parts, group - 1)),
            dma((2, parts, group - 1)), dma((2, parts, group - 1)), dma((2, parts)), dma((1 + parts,)),
            dma((group - 1,)), dma((group - 1,)), dma((8,)), dma((4, n_slots)), dma((4, n_slots)), dma((6,)), dma((6,)),
        ],
        compiler_params=pltpu.CompilerParams(
            collective_id=0, has_side_effects=True, vmem_limit_bytes=67043328
        ),
    )(iterate, source_term, conductivity)


def solution(mesh):
    tiled = P("tm", "space", None, None, None)
    in_specs = (tiled, tiled, P("space", None, None, None))
    body = functools.partial(shards, mesh.shape["tm"], mesh.shape["space"])
    return jax.shard_map(
        body, mesh=mesh, in_specs=in_specs, out_specs=(tiled, tiled), check_vma=False
    )
```
